128 devices in a mesh: dp: 4 (over z_hi, core), ctx: 32 (over z_lo, x, y).
Axes of the slice: x: 4, y: 4, z: 4 (z_hi: 2, z_lo: 2; z = z_hi * 2 + z_lo), core: 2. Of those that a mesh axis runs over, the one named last changes fastest.
Arguments:
- queries: bfloat16 [32768, 1536], P(('dp', 'ctx')), parts along dimension 0, may hold values from -53 to 53
- keys: bfloat16 [32768, 1536], P(('dp', 'ctx')), parts along dimension 0, may hold values from -6 to 6
- values: bfloat16 [32768, 1536], P(('dp', 'ctx')), parts along dimension 0, may hold values from -6 to 6
- grad_out: bfloat16 [32768, 1536], P(('dp', 'ctx')), parts along dimension 0, may hold values from -6 to 6
- summary_lists: int32 [256, 4], P('dp'), parts along dimension 0, may hold values from 0 to 7, as said below
Outputs:
- attended: bfloat16 [32768, 1536], P(('dp', 'ctx')), parts along dimension 0
- grad_queries: bfloat16 [32768, 1536], P(('dp', 'ctx')), parts along dimension 0
- grad_keys: bfloat16 [32768, 1536], P(('dp', 'ctx')), parts along dimension 0
- grad_values: bfloat16 [32768, 1536], P(('dp', 'ctx')), parts along dimension 0
The draws below stay inside these ranges and needn't reach their ends.
There are 4 independent parts, one for each index of `dp`. The reference program is written for one: setup_inputs(seed, part) draws one part's arguments, and reference() takes and returns one part's arrays. A program takes and returns all parts, laid end to end along the dimension named above; each array names one. Nothing has to cross between parts.
Inputs may be any that keep to these rules, and one draw needn't show every extreme that they name: `summary_lists`: each row names 4 different summary numbers.
All inputs are finite; a program needn't handle non-finite values.
Results may differ from the reference program's by a relative error of at most 0.019.
Values may be sent and summed in bfloat16 or wider, within the bound.
No kernel may reach another device: no remote copies, remote signals or barrier semaphores. Data moves between devices by JAX's collectives and lax.ppermute only.
A program may use at most 192 MiB of HBM per device.

```python
import jax
import jax.numpy as jnp
from jax import lax

H = 12
HS = 128
BLK = 128
SUMS = 8
PICKS = 4
TOK_DEV = 256
TOKENS = 8192
NB = 64
STRIDE = 8
N_CTX = 32


def draw_queries(key, part):
    drawn = jax.random.normal(jax.random.fold_in(key, 1), (TOKENS, H * HS), jnp.float32)
    return jnp.clip(drawn, -6.0, 6.0).astype(jnp.bfloat16)


def draw_keys(key, part):
    drawn = jax.random.normal(jax.random.fold_in(key, 2), (TOKENS, H * HS), jnp.float32)
    return jnp.clip(drawn, -6.0, 6.0).astype(jnp.bfloat16)


def draw_summary_lists(key, part):
    row_keys = jax.random.split(jax.random.fold_in(key, 5), NB)

    def one_row(row_key):
        return jax.random.permutation(row_key, SUMS)[:PICKS]
    return jax.vmap(one_row)(row_keys).astype(jnp.int32)


def block_levels(stream_key, extent, pieces, least, high):
    factor_of, own = 1.0, jax.random.fold_in(stream_key, 6)
    for axis_at, parts in pieces:
        draws = jnp.exp(jax.random.uniform(jax.random.fold_in(own, axis_at), (parts,), jnp.float32, least / len(pieces), high / len(pieces)))
        factor_of = factor_of * jnp.repeat(draws, extent[axis_at] // parts).reshape([-1 if axis == axis_at else 1 for axis in range(len(extent))])
    return factor_of


def gaussian(own_key, extent, spread, bound, pieces=(), kind=jnp.bfloat16):
    values = jax.random.normal(own_key, extent, jnp.float32) * spread
    if len(pieces) > 0:
        values = block_levels(own_key, extent, pieces, -0.22, 0.18) * values
    return jnp.clip(values, min=-bound, max=bound).astype(kind)


def setup_inputs(seed: int = 0, part: int = 0) -> dict:
    key_of = jax.random.split(jax.random.key(seed), 6)
    own_keys = jax.random.split(jax.random.fold_in(key_of[5], part), 6)
    queries = draw_queries(jax.random.fold_in(jax.random.fold_in(key_of[5], part), 71), part)
    keys = draw_keys(jax.random.fold_in(jax.random.fold_in(key_of[5], part), 71), part)
    values = gaussian(own_keys[2], (TOKENS, H * HS), 1.0, 6.0, ((0, 32),))
    grad_out = gaussian(own_keys[3], (TOKENS, H * HS), 1.0, 6.0, ((0, 32),))
    summary_lists = draw_summary_lists(jax.random.fold_in(jax.random.fold_in(key_of[5], part), 71), part)
    return dict(queries=queries, keys=keys, values=values, grad_out=grad_out, summary_lists=summary_lists)


def storage_of_doc():
    half_rows = TOK_DEV // 2
    position = jnp.arange(TOKENS, dtype=jnp.int32)
    span_id = position // half_rows
    within = position % half_rows
    owner_dev = jnp.where(span_id < N_CTX, span_id, 2 * N_CTX - 1 - span_id)
    offset = jnp.where(span_id < N_CTX, within, half_rows + within)
    return (owner_dev * TOK_DEV + offset).astype(jnp.int32)


def doc_of_storage():
    half_rows = TOK_DEV // 2
    row_ids = jnp.arange(TOKENS, dtype=jnp.int32)
    owner_dev = row_ids // TOK_DEV
    within = row_ids % TOK_DEV
    first = owner_dev * half_rows + within
    second = (2 * N_CTX - 1 - owner_dev) * half_rows + within - half_rows
    return jnp.where(within < half_rows, first, second).astype(jnp.int32)


def attend_block(query_blk, key_rows, value_rows, grad_blk, visible, scale):
    query_f = query_blk.astype(jnp.float32)
    key_f = key_rows.astype(jnp.float32)
    value_f = value_rows.astype(jnp.float32)
    grad_f = grad_blk.astype(jnp.float32)
    scores = jnp.einsum("gqhd,gkhd->ghqk", query_f, key_f) * scale
    scores = jnp.where(visible[:, None], scores, -1e30)
    highest = jnp.max(scores, axis=-1, keepdims=True)
    weights = jnp.where(visible[:, None], jnp.exp(scores - highest), 0.0)
    probs = weights / jnp.sum(weights, axis=-1, keepdims=True)
    probs_low = probs.astype(jnp.bfloat16)
    attended = jnp.einsum("ghqk,gkhd->gqhd", probs_low.astype(jnp.float32), value_f).astype(jnp.bfloat16)
    delta = jnp.sum(grad_f * attended.astype(jnp.float32), axis=-1)
    dprob = jnp.einsum("gqhd,gkhd->ghqk", grad_f, value_f)
    dscore = (probs * (dprob - jnp.transpose(delta, (0, 2, 1))[..., None])).astype(jnp.bfloat16)
    dscore_f = dscore.astype(jnp.float32)
    grad_query = (jnp.einsum("ghqk,gkhd->gqhd", dscore_f, key_f) * scale).astype(jnp.bfloat16)
    grad_key = jnp.einsum("ghqk,gqhd->gkhd", dscore_f, query_f) * scale
    grad_value = jnp.einsum("ghqk,gqhd->gkhd", probs_low.astype(jnp.float32), grad_f)
    return attended, grad_query, grad_key, grad_value


def reference(queries, keys, values, grad_out, summary_lists):
    feat_width = queries.shape[1]
    scale = HS ** -0.5
    kcount = 2 + PICKS
    gather_rows = storage_of_doc()

    def to_doc(array):
        return jnp.take(array, gather_rows, axis=0).reshape(NB, BLK, H, HS)

    doc_queries = to_doc(queries)
    doc_keys = to_doc(keys)
    doc_values = to_doc(values)
    doc_grads = to_doc(grad_out)
    causal = jnp.arange(BLK)[:, None] >= jnp.arange(BLK)[None, :]
    kinds = jnp.arange(kcount)[:, None, None]

    def step(carry, block_id):
        acc_keys, acc_values = carry
        picks = (summary_lists[block_id] * STRIDE + STRIDE - 1).astype(jnp.int32)
        previous = jnp.maximum(block_id - 1, 0)
        key_ids = jnp.concatenate([previous[None], block_id[None], picks]).astype(jnp.int32)
        live = jnp.concatenate([(block_id >= 1)[None], jnp.ones((1,), bool), picks < block_id - 1])
        visible = jnp.where(kinds == 1, causal[None], live[:, None, None])
        visible = jnp.transpose(visible, (1, 0, 2)).reshape(BLK, kcount * BLK)
        key_rows = doc_keys[key_ids].reshape(kcount * BLK, H, HS)
        value_rows = doc_values[key_ids].reshape(kcount * BLK, H, HS)
        attended, grad_query, grad_key, grad_value = attend_block(
            doc_queries[block_id][None], key_rows[None], value_rows[None], doc_grads[block_id][None], visible[None], scale)
        acc_keys = acc_keys.at[key_ids].add(grad_key.reshape(kcount, BLK, H, HS))
        acc_values = acc_values.at[key_ids].add(grad_value.reshape(kcount, BLK, H, HS))
        return (acc_keys, acc_values), (attended[0], grad_query[0])

    start = (jnp.zeros((NB, BLK, H, HS), jnp.float32), jnp.zeros((NB, BLK, H, HS), jnp.float32))
    (acc_keys, acc_values), (outs, grads_q) = lax.scan(step, start, jnp.arange(NB, dtype=jnp.int32))
    back_rows = doc_of_storage()

    def to_storage(array):
        return jnp.take(array.reshape(TOKENS, feat_width), back_rows, axis=0)

    return (to_storage(outs), to_storage(grads_q),
            to_storage(acc_keys.astype(jnp.bfloat16)), to_storage(acc_values.astype(jnp.bfloat16)))
```

```python
import jax
import jax.numpy as jnp
from jax import lax
from jax.experimental import pallas as pl
from jax.experimental.pallas import tpu as pltpu
from jax.sharding import PartitionSpec as P

H = 12
HS = 128
BLK = 128
SUMS = 8
PICKS = 4
N_CTX = 32
RING = 4
GROUPS = N_CTX // RING
HEADS = H // RING
COLS = HEADS * HS
EDGE = SUMS
OWN = SUMS + 1
SLOTS = OWN + 2 * RING
SCALE = HS ** (-0.5)
NEG = -1e30
BF16 = jnp.bfloat16
F32 = jnp.float32


RING_GROUPS = [[RING * c + y for y in range(RING)] for c in range(GROUPS)]
SHIFTS = [(0, 0), (1, 0), (3, 0), (2, 0), (0, 1), (1, 1), (3, 1), (2, 1)]


def summary_y(c):
    return 3 * (c % 2)


def edge_y(c):
    return 3 - 3 * (c % 2)


def summary_of(c):
    return (c - 1) // 2 if c % 2 else 7 - c // 2


def uses(c, source):
    return 8 * summary_of(source) + 9 <= 63 - 4 * c


def moved(c, shift):
    return 4 * ((c // 4 + shift[1]) % 2) + (c % 4 + shift[0]) % 4


def scatter_pairs(k):
    pairs = []
    for c in range(GROUPS):
        if k < RING:
            pairs.append((4 * c + summary_y(c), 4 * c + (summary_y(c) + k) % 4))
        pairs.append((4 * c + edge_y(c), 4 * (c ^ 1) + (edge_y(c) + k - 1) % 4))
    return pairs


def return_pairs(k):
    pairs = []
    for c in range(GROUPS):
        for end in (summary_y(c), edge_y(c)):
            pairs.append((4 * c + (end + k) % 4, 4 * c + end))
    return pairs


def spread_pairs(shift):
    return [
        (4 * c + y, 4 * moved(c, shift) + y)
        for c in range(GROUPS)
        for y in range(RING)
        if uses(moved(c, shift), c)
    ]


def reduce_pairs(shift):
    return [
        (4 * c + y, 4 * moved(c, shift) + y)
        for c in range(GROUPS)
        for y in range(RING)
        if uses(c, moved(c, shift))
    ]


def edge_pairs():
    return [(4 * c + y, 4 * (c ^ 1) + y) for c in range(GROUPS) for y in range(RING)]


def payload_kernel(place, keys, values, *outs):
    y = place[0] % 4
    odd = (place[0] // 4) % 2
    is_summary = (y == 3) == (odd == 1)
    first = jnp.where(is_summary, y, y + 3)
    for k, out in enumerate(outs):
        start = pl.multiple_of(((first + k) % 4) * COLS, COLS)
        out[0] = keys[:, pl.ds(start, COLS)]
        out[1] = values[:, pl.ds(start, COLS)]


def payloads(place, keys, values):
    half = pl.BlockSpec((BLK, H * HS), lambda i, place: (jnp.where(place[0] % 4 == 3, 0, 1), 0))
    piece = jax.ShapeDtypeStruct((2, BLK, COLS), BF16)
    return pl.pallas_call(
        payload_kernel,
        grid_spec=pltpu.PrefetchScalarGridSpec(
            num_scalar_prefetch=1,
            grid=(1,),
            in_specs=[half, half],
            out_specs=[pl.BlockSpec((2, BLK, COLS), lambda i, place: (0, 0, 0))] * 5,
        ),
        out_shape=[piece] * 5,
        name="payloads",
    )(place, keys, values)


def pack_kernel(queries, grads, keys, values, out):
    out[0, 0] = queries[...]
    out[0, 1] = grads[...]
    out[0, 2] = keys[...]
    out[0, 3] = values[...]


def pack(queries, grads, keys, values):
    rows = queries.shape[0]
    return pl.pallas_call(
        pack_kernel,
        grid=(RING,),
        in_specs=[pl.BlockSpec((rows, COLS), lambda i: (0, i))] * 4,
        out_specs=pl.BlockSpec((1, 4, rows, COLS), lambda i: (i, 0, 0, 0)),
        out_shape=jax.ShapeDtypeStruct((RING, 4, rows, COLS), BF16),
        name="pack",
    )(queries, grads, keys, values)


def summary_slot(c):
    return jnp.where(c % 2 == 1, (c - 1) // 2, 7 - c // 2)


def nt(a, b):
    return lax.dot_general(a, b, (((1,), (1,)), ((), ())), preferred_element_type=F32)


def nn(a, b):
    return lax.dot_general(a, b, (((1,), (0,)), ((), ())), preferred_element_type=F32)


def attend_kernel(place, lists, recv, *refs):
    spread, edge = refs[:8], refs[8]
    out, parts, edge_out = refs[9], refs[10:18], refs[18]
    bank, grad_bank = refs[19], refs[20]
    c = place[0] // 4
    x, z = c % 4, c // 4

    def slot_at(shift, sign):
        return summary_slot(4 * ((z + shift[1]) % 2) + (x + 4 + sign * shift[0]) % 4)

    for shift, piece in zip(SHIFTS, spread):
        bank[slot_at(shift, -1)] = piece[...]
    bank[EDGE] = edge[...]
    for g in range(8):
        y, row = (g, 0) if g < 4 else (7 - g, BLK)
        for kind in range(2):
            bank[OWN + g, kind] = recv[y, 2 + kind, row : row + BLK, :]

    def clear(slot, carry):
        grad_bank[slot] = jnp.zeros(grad_bank.shape[1:], F32)
        return carry

    lax.fori_loop(0, SLOTS, clear, 0)
    causal = lax.broadcasted_iota(jnp.int32, (BLK, BLK), 0) >= lax.broadcasted_iota(
        jnp.int32, (BLK, BLK), 1
    )

    def one_block(g, carry):
        lower = g < 4
        y = jnp.where(lower, g, 7 - g)
        row = pl.multiple_of(jnp.where(lower, 0, BLK), BLK)
        block = jnp.where(lower, 4 * c + g, 56 - 4 * c + g)
        outside = jnp.where(
            lower,
            jnp.where(c % 2 == 0, jnp.maximum(c // 2 - 1, 0), EDGE),
            jnp.where(c % 2 == 0, EDGE, (13 - c) // 2),
        )
        prev = jnp.where(g % 4 == 0, outside, OWN + g - 1)
        slots = [prev, OWN + g]
        bias = [jnp.where(block >= 1, 0.0, NEG), None]
        for p in range(PICKS):
            pick = lists[block, p]
            slots.append(pick)
            bias.append(jnp.where(8 * pick + 7 < block - 1, 0.0, NEG))
        for h in range(HEADS):
            cols = slice(h * HS, (h + 1) * HS)
            query = recv[y, 0, pl.ds(row, BLK), cols]
            grad = recv[y, 1, pl.ds(row, BLK), cols]
            key_rows = jnp.concatenate([bank[s, 0, :, cols] for s in slots], axis=0)
            value_rows = jnp.concatenate([bank[s, 1, :, cols] for s in slots], axis=0)
            scores = nt(query, key_rows) * SCALE
            pieces = []
            for i in range(2 + PICKS):
                piece = scores[:, i * BLK : (i + 1) * BLK]
                if bias[i] is None:
                    pieces.append(jnp.where(causal, piece, NEG))
                else:
                    pieces.append(piece + bias[i])
            scores = jnp.concatenate(pieces, axis=1)
            weights = jnp.exp(scores - jnp.max(scores, axis=1, keepdims=True))
            probs = weights * (1.0 / jnp.sum(weights, axis=1, keepdims=True))
            probs_low = probs.astype(BF16)
            attended = nn(probs_low, value_rows).astype(BF16)
            out[y, 0, pl.ds(row, BLK), cols] = attended
            delta = jnp.sum(grad.astype(F32) * attended.astype(F32), axis=1, keepdims=True)
            dprob = nt(grad, value_rows)
            dscore = (probs * (dprob - delta)).astype(BF16)
            out[y, 1, pl.ds(row, BLK), cols] = (nn(dscore, key_rows) * SCALE).astype(BF16)
            grad_keys = nn(query.T, dscore)
            grad_values = nn(grad.T, probs_low)
            for i, s in enumerate(slots):
                at = slice(i * BLK, (i + 1) * BLK)
                grad_bank[s, 0, h] += grad_keys[:, at]
                grad_bank[s, 1, h] += grad_values[:, at]
        return carry

    lax.fori_loop(0, 8, one_block, 0)

    def taken(slot, kind, h):
        total = grad_bank[slot, kind, h]
        if kind == 0:
            total = total * SCALE
        return total.T.astype(BF16)

    def finish(g, carry):
        lower = g < 4
        y = jnp.where(lower, g, 7 - g)
        row = pl.multiple_of(jnp.where(lower, 0, BLK), BLK)
        for kind in range(2):
            for h in range(HEADS):
                cols = slice(h * HS, (h + 1) * HS)
                out[y, 2 + kind, pl.ds(row, BLK), cols] = taken(OWN + g, kind, h)
        return carry

    lax.fori_loop(0, 8, finish, 0)
    for kind in range(2):
        for h in range(HEADS):
            cols = slice(h * HS, (h + 1) * HS)
            edge_out[kind, :, cols] = taken(EDGE, kind, h)
            for shift, part in zip(SHIFTS, parts):
                part[kind, :, cols] = taken(slot_at(shift, 1), kind, h)


def attend(place, lists, recv, spread, edge):
    vmem = pl.BlockSpec(memory_space=pltpu.VMEM)
    smem = pl.BlockSpec(memory_space=pltpu.SMEM)
    piece = jax.ShapeDtypeStruct((2, BLK, COLS), BF16)
    outs = pl.pallas_call(
        attend_kernel,
        in_specs=[smem, smem, vmem] + [vmem] * 9,
        out_specs=[vmem] * 10,
        out_shape=[jax.ShapeDtypeStruct(recv.shape, BF16)] + [piece] * 9,
        scratch_shapes=[
            pltpu.VMEM((SLOTS, 2, BLK, COLS), BF16),
            pltpu.VMEM((SLOTS, 2, HEADS, HS, BLK), F32),
        ],
        name="attend",
    )(place, lists, recv, *spread, edge)
    return outs[0], outs[1:9], outs[9]


def unpack_kernel(place, recv, own, one, two, three, out, grad_q, grad_k, grad_v):
    y = place[0] % 4
    step = pl.program_id(0)
    out[...] = recv[0, 0]
    grad_q[...] = recv[0, 1]
    grad_k[...] = recv[0, 2]
    grad_v[...] = recv[0, 3]
    for end, row in ((3, 0), (0, BLK)):
        for i, extra in enumerate((own, one, two, three)):

            @pl.when((y == end) & (step == (y + i) % 4))
            def _():
                for kind, grad in ((0, grad_k), (1, grad_v)):
                    total = recv[0, 2 + kind, row : row + BLK].astype(F32)
                    grad[row : row + BLK] = (total + extra[kind].astype(F32)).astype(BF16)


def unpack(place, recv, extras):
    rows = recv.shape[2]
    whole = pl.BlockSpec((2, BLK, COLS), lambda i, place: (0, 0, 0))
    return pl.pallas_call(
        unpack_kernel,
        grid_spec=pltpu.PrefetchScalarGridSpec(
            num_scalar_prefetch=1,
            grid=(RING,),
            in_specs=[pl.BlockSpec((1, 4, rows, COLS), lambda i, place: (i, 0, 0, 0))]
            + [whole] * 4,
            out_specs=[pl.BlockSpec((rows, COLS), lambda i, place: (0, i))] * 4,
        ),
        out_shape=[jax.ShapeDtypeStruct((rows, H * HS), BF16)] * 4,
        name="unpack",
    )(place, recv, *extras)


def on_device(queries, keys, values, grad_out, summary_lists):
    here = lax.axis_index("ctx").astype(jnp.int32)
    place = here[None]
    c, y = here // 4, here % 4
    from_summary = (y - 3 * (c % 2)) % 4
    from_edge = (y - 3 + 3 * (c % 2)) % 4

    pays = payloads(place, keys, values)
    got = [pays[0]] + [lax.ppermute(pays[k], "ctx", scatter_pairs(k)) for k in range(1, 5)]
    sent = pack(queries, grad_out, keys, values)
    recv = lax.all_to_all(sent, "ctx", 0, 0, axis_index_groups=RING_GROUPS)
    summary, edge = got[0], got[1]
    for k in range(1, 4):
        summary = jnp.where(from_summary == k, got[k], summary)
        edge = jnp.where(from_summary == k, got[k + 1], edge)
    spread = [summary] + [lax.ppermute(summary, "ctx", spread_pairs(s)) for s in SHIFTS[1:]]

    back, parts, edge_grad = attend(place, summary_lists, recv, spread, edge)

    total = parts[0].astype(F32)
    for part, shift in zip(parts[1:], SHIFTS[1:]):
        total = total + lax.ppermute(part, "ctx", reduce_pairs(shift)).astype(F32)
    total = total.astype(BF16)
    edge_total = lax.ppermute(edge_grad, "ctx", edge_pairs())
    home = lax.all_to_all(back, "ctx", 0, 0, axis_index_groups=RING_GROUPS)
    extras = [jnp.where(from_summary == 0, total, edge_total)]
    for k in range(1, 4):
        mine = jnp.where(from_summary == k, total, edge_total)
        extras.append(lax.ppermute(mine, "ctx", return_pairs(k)))
    return tuple(unpack(place, home, extras))


def solution(mesh):
    rows = P(("dp", "ctx"), None)
    return jax.shard_map(
        on_device,
        mesh=mesh,
        in_specs=(rows, rows, rows, rows, P("dp", None)),
        out_specs=(rows, rows, rows, rows),
        check_vma=False,
    )
```

```python
import jax
import jax.numpy as jnp
from jax import lax
from jax.experimental import pallas as pl
from jax.experimental.pallas import tpu as pltpu
from jax.sharding import PartitionSpec as P

H = 12
HS = 128
BLK = 128
SUMS = 8
PICKS = 4
N_CTX = 32
RING = 4
GROUPS = N_CTX // RING
HEADS = H // RING
COLS = HEADS * HS
EDGE = SUMS
OWN = SUMS + 1
SLOTS = OWN + 2 * RING
SCALE = HS ** (-0.5)
NEG = -1e30
BF16 = jnp.bfloat16
F32 = jnp.float32


RING_GROUPS = [[RING * c + y for y in range(RING)] for c in range(GROUPS)]
SHIFTS = [(0, 0), (1, 0), (3, 0), (2, 0), (0, 1), (1, 1), (3, 1), (2, 1)]


def summary_y(c):
    return 3 * (c % 2)


def edge_y(c):
    return 3 - 3 * (c % 2)


def summary_of(c):
    return (c - 1) // 2 if c % 2 else 7 - c // 2


def uses(c, source):
    return 8 * summary_of(source) + 9 <= 63 - 4 * c


def moved(c, shift):
    return 4 * ((c // 4 + shift[1]) % 2) + (c % 4 + shift[0]) % 4


def return_pairs(k):
    pairs = []
    for c in range(GROUPS):
        for end in (summary_y(c), edge_y(c)):
            pairs.append((4 * c + (end + k) % 4, 4 * c + end))
    return pairs


def spread_pairs(shift):
    return [
        (4 * c + y, 4 * moved(c, shift) + y)
        for c in range(GROUPS)
        for y in range(RING)
        if uses(moved(c, shift), c)
    ]


def reduce_pairs(shift):
    return [
        (4 * c + y, 4 * moved(c, shift) + y)
        for c in range(GROUPS)
        for y in range(RING)
        if uses(c, moved(c, shift))
    ]


def edge_pairs():
    return [(4 * c + y, 4 * (c ^ 1) + y) for c in range(GROUPS) for y in range(RING)]


def pack_kernel(first, second, out):
    out[0, 0] = first[...]
    out[0, 1] = second[...]


def pack(first, second):
    rows = first.shape[0]
    return pl.pallas_call(
        pack_kernel,
        grid=(RING,),
        in_specs=[pl.BlockSpec((rows, COLS), lambda i: (0, i))] * 2,
        out_specs=pl.BlockSpec((1, 2, rows, COLS), lambda i: (i, 0, 0, 0)),
        out_shape=jax.ShapeDtypeStruct((RING, 2, rows, COLS), BF16),
        name="pack",
    )(first, second)


def summary_slot(c):
    return jnp.where(c % 2 == 1, (c - 1) // 2, 7 - c // 2)


def nt(a, b):
    return lax.dot_general(a, b, (((1,), (1,)), ((), ())), preferred_element_type=F32)


def nn(a, b):
    return lax.dot_general(a, b, (((1,), (0,)), ((), ())), preferred_element_type=F32)


def attend_kernel(place, lists, recv_kv, recv, *refs):
    spread, edge = refs[:8], refs[8]
    out, parts, edge_out = refs[9], refs[10:18], refs[18]
    bank, grad_bank = refs[19], refs[20]
    c = place[0] // 4
    x, z = c % 4, c // 4

    def slot_at(shift, sign):
        return summary_slot(4 * ((z + shift[1]) % 2) + (x + 4 + sign * shift[0]) % 4)

    for shift, piece in zip(SHIFTS, spread):
        bank[slot_at(shift, -1)] = piece[...]
    bank[EDGE] = edge[...]
    for g in range(8):
        y, row = (g, 0) if g < 4 else (7 - g, BLK)
        for kind in range(2):
            bank[OWN + g, kind] = recv_kv[y, kind, row : row + BLK, :]

    def clear(slot, carry):
        grad_bank[slot] = jnp.zeros(grad_bank.shape[1:], F32)
        return carry

    lax.fori_loop(0, SLOTS, clear, 0)
    causal = lax.broadcasted_iota(jnp.int32, (BLK, BLK), 0) >= lax.broadcasted_iota(
        jnp.int32, (BLK, BLK), 1
    )

    def one_block(g, carry):
        lower = g < 4
        y = jnp.where(lower, g, 7 - g)
        row = pl.multiple_of(jnp.where(lower, 0, BLK), BLK)
        block = jnp.where(lower, 4 * c + g, 56 - 4 * c + g)
        outside = jnp.where(
            lower,
            jnp.where(c % 2 == 0, jnp.maximum(c // 2 - 1, 0), EDGE),
            jnp.where(c % 2 == 0, EDGE, (13 - c) // 2),
        )
        prev = jnp.where(g % 4 == 0, outside, OWN + g - 1)
        slots = [prev, OWN + g]
        bias = [jnp.where(block >= 1, 0.0, NEG), None]
        for p in range(PICKS):
            pick = lists[block, p]
            slots.append(pick)
            bias.append(jnp.where(8 * pick + 7 < block - 1, 0.0, NEG))
        for h in range(HEADS):
            cols = slice(h * HS, (h + 1) * HS)
            query = recv[y, 0, pl.ds(row, BLK), cols]
            grad = recv[y, 1, pl.ds(row, BLK), cols]
            key_rows = jnp.concatenate([bank[s, 0, :, cols] for s in slots], axis=0)
            value_rows = jnp.concatenate([bank[s, 1, :, cols] for s in slots], axis=0)
            scores = nt(query, key_rows) * SCALE
            pieces = []
            for i in range(2 + PICKS):
                piece = scores[:, i * BLK : (i + 1) * BLK]
                if bias[i] is None:
                    pieces.append(jnp.where(causal, piece, NEG))
                else:
                    pieces.append(piece + bias[i])
            scores = jnp.concatenate(pieces, axis=1)
            weights = jnp.exp(scores - jnp.max(scores, axis=1, keepdims=True))
            probs = weights * (1.0 / jnp.sum(weights, axis=1, keepdims=True))
            probs_low = probs.astype(BF16)
            attended = nn(probs_low, value_rows).astype(BF16)
            out[y, 0, pl.ds(row, BLK), cols] = attended
            delta = jnp.sum(grad.astype(F32) * attended.astype(F32), axis=1, keepdims=True)
            dprob = nt(grad, value_rows)
            dscore = (probs * (dprob - delta)).astype(BF16)
            out[y, 1, pl.ds(row, BLK), cols] = (nn(dscore, key_rows) * SCALE).astype(BF16)
            grad_keys = nn(query.T, dscore)
            grad_values = nn(grad.T, probs_low)
            for i, s in enumerate(slots):
                at = slice(i * BLK, (i + 1) * BLK)
                grad_bank[s, 0, h] += grad_keys[:, at]
                grad_bank[s, 1, h] += grad_values[:, at]
        return carry

    lax.fori_loop(0, 8, one_block, 0)

    def taken(slot, kind, h):
        total = grad_bank[slot, kind, h]
        if kind == 0:
            total = total * SCALE
        return total.T.astype(BF16)

    def finish(g, carry):
        lower = g < 4
        y = jnp.where(lower, g, 7 - g)
        row = pl.multiple_of(jnp.where(lower, 0, BLK), BLK)
        for kind in range(2):
            for h in range(HEADS):
                cols = slice(h * HS, (h + 1) * HS)
                out[y, 2 + kind, pl.ds(row, BLK), cols] = taken(OWN + g, kind, h)
        return carry

    lax.fori_loop(0, 8, finish, 0)
    for kind in range(2):
        for h in range(HEADS):
            cols = slice(h * HS, (h + 1) * HS)
            edge_out[kind, :, cols] = taken(EDGE, kind, h)
            for shift, part in zip(SHIFTS, parts):
                part[kind, :, cols] = taken(slot_at(shift, 1), kind, h)


def attend(place, lists, recv_kv, recv, spread, edge):
    vmem = pl.BlockSpec(memory_space=pltpu.VMEM)
    smem = pl.BlockSpec(memory_space=pltpu.SMEM)
    piece = jax.ShapeDtypeStruct((2, BLK, COLS), BF16)
    outs = pl.pallas_call(
        attend_kernel,
        in_specs=[smem, smem] + [vmem] * 11,
        out_specs=[vmem] * 10,
        out_shape=[jax.ShapeDtypeStruct((RING, 4, 2 * BLK, COLS), BF16)] + [piece] * 9,
        scratch_shapes=[
            pltpu.VMEM((SLOTS, 2, BLK, COLS), BF16),
            pltpu.VMEM((SLOTS, 2, HEADS, HS, BLK), F32),
        ],
        name="attend",
    )(place, lists, recv_kv, recv, *spread, edge)
    return outs[0], outs[1:9], outs[9]


def unpack_kernel(place, recv, own, one, two, three, out, grad_q, grad_k, grad_v):
    y = place[0] % 4
    step = pl.program_id(0)
    out[...] = recv[0, 0]
    grad_q[...] = recv[0, 1]
    grad_k[...] = recv[0, 2]
    grad_v[...] = recv[0, 3]
    for end, row in ((3, 0), (0, BLK)):
        for i, extra in enumerate((own, one, two, three)):

            @pl.when((y == end) & (step == (y + i) % 4))
            def _():
                for kind, grad in ((0, grad_k), (1, grad_v)):
                    total = recv[0, 2 + kind, row : row + BLK].astype(F32)
                    grad[row : row + BLK] = (total + extra[kind].astype(F32)).astype(BF16)


def unpack(place, recv, extras):
    rows = recv.shape[2]
    whole = pl.BlockSpec((2, BLK, COLS), lambda i, place: (0, 0, 0))
    return pl.pallas_call(
        unpack_kernel,
        grid_spec=pltpu.PrefetchScalarGridSpec(
            num_scalar_prefetch=1,
            grid=(RING,),
            in_specs=[pl.BlockSpec((1, 4, rows, COLS), lambda i, place: (i, 0, 0, 0))]
            + [whole] * 4,
            out_specs=[pl.BlockSpec((rows, COLS), lambda i, place: (0, i))] * 4,
        ),
        out_shape=[jax.ShapeDtypeStruct((rows, H * HS), BF16)] * 4,
        name="unpack",
    )(place, recv, *extras)


def on_device(queries, keys, values, grad_out, summary_lists):
    here = lax.axis_index("ctx").astype(jnp.int32)
    place = here[None]
    c, y = here // 4, here % 4
    from_summary = (y - 3 * (c % 2)) % 4

    def ring_exchange(sent):
        return lax.all_to_all(sent, "ctx", 0, 0, axis_index_groups=RING_GROUPS)

    recv_kv = ring_exchange(pack(keys, values))
    recv = ring_exchange(pack(queries, grad_out))
    odd = c % 2 == 1
    ends = recv_kv[3, :, :BLK], recv_kv[0, :, BLK:]
    summary = jnp.where(odd, ends[0], ends[1])
    edge = lax.ppermute(jnp.where(odd, ends[1], ends[0]), "ctx", edge_pairs())
    spread = [summary] + [lax.ppermute(summary, "ctx", spread_pairs(s)) for s in SHIFTS[1:]]

    back, parts, edge_grad = attend(place, summary_lists, recv_kv, recv, spread, edge)

    total = parts[0].astype(F32)
    for part, shift in zip(parts[1:], SHIFTS[1:]):
        total = total + lax.ppermute(part, "ctx", reduce_pairs(shift)).astype(F32)
    total = total.astype(BF16)
    edge_total = lax.ppermute(edge_grad, "ctx", edge_pairs())
    home = ring_exchange(back)
    extras = [jnp.where(from_summary == 0, total, edge_total)]
    for k in range(1, 4):
        mine = jnp.where(from_summary == k, total, edge_total)
        extras.append(lax.ppermute(mine, "ctx", return_pairs(k)))
    return tuple(unpack(place, home, extras))


def solution(mesh):
    rows = P(("dp", "ctx"), None)
    return jax.shard_map(
        on_device,
        mesh=mesh,
        in_specs=(rows, rows, rows, rows, P("dp", None)),
        out_specs=(rows, rows, rows, rows),
        check_vma=False,
    )
```

```python
import jax
import jax.numpy as jnp
from jax import lax
from jax.experimental import pallas as pl
from jax.experimental.pallas import tpu as pltpu
from jax.sharding import PartitionSpec as P

H = 12
HS = 128
BLK = 128
SUMS = 8
PICKS = 4
N_CTX = 32
RING = 4
GROUPS = N_CTX // RING
HEADS = H // RING
COLS = HEADS * HS
EDGE = SUMS
OWN = SUMS + 1
SLOTS = OWN + 2 * RING
SCALE = HS ** (-0.5)
NEG = -1e30
BF16 = jnp.bfloat16
F32 = jnp.float32


RING_GROUPS = [[RING * c + y for y in range(RING)] for c in range(GROUPS)]
SHIFTS = [(0, 0), (1, 0), (3, 0), (2, 0), (0, 1), (1, 1), (3, 1), (2, 1)]


def summary_y(c):
    return 3 * (c % 2)


def edge_y(c):
    return 3 - 3 * (c % 2)


def summary_of(c):
    return (c - 1) // 2 if c % 2 else 7 - c // 2


def uses(c, source):
    return 8 * summary_of(source) + 9 <= 63 - 4 * c


def moved(c, shift):
    return 4 * ((c // 4 + shift[1]) % 2) + (c % 4 + shift[0]) % 4


def return_pairs(k):
    pairs = []
    for c in range(GROUPS):
        for end in (summary_y(c), edge_y(c)):
            pairs.append((4 * c + (end + k) % 4, 4 * c + end))
    return pairs


def spread_pairs(shift):
    return [
        (4 * c + y, 4 * moved(c, shift) + y)
        for c in range(GROUPS)
        for y in range(RING)
        if uses(moved(c, shift), c)
    ]


def reduce_pairs(shift):
    return [
        (4 * c + y, 4 * moved(c, shift) + y)
        for c in range(GROUPS)
        for y in range(RING)
        if uses(c, moved(c, shift))
    ]


def edge_pairs():
    return [(4 * c + y, 4 * (c ^ 1) + y) for c in range(GROUPS) for y in range(RING)]


def pack_kernel(first, second, out):
    out[0, 0] = first[...]
    out[0, 1] = second[...]


def pack(first, second):
    rows = first.shape[0]
    return pl.pallas_call(
        pack_kernel,
        grid=(RING,),
        in_specs=[pl.BlockSpec((rows, COLS), lambda i: (0, i))] * 2,
        out_specs=pl.BlockSpec((1, 2, rows, COLS), lambda i: (i, 0, 0, 0)),
        out_shape=jax.ShapeDtypeStruct((RING, 2, rows, COLS), BF16),
        name="pack",
    )(first, second)


def summary_slot(c):
    return jnp.where(c % 2 == 1, (c - 1) // 2, 7 - c // 2)


def nt(a, b):
    return lax.dot_general(a, b, (((1,), (1,)), ((), ())), preferred_element_type=F32)


def nn(a, b):
    return lax.dot_general(a, b, (((1,), (0,)), ((), ())), preferred_element_type=F32)


def attend_kernel(place, lists, recv_kv, recv, *refs):
    spread, edge = refs[:8], refs[8]
    out, parts, edge_out = refs[9], refs[10:18], refs[18]
    bank, grad_bank = refs[19], refs[20]
    c = place[0] // 4
    x, z = c % 4, c // 4

    def slot_at(shift, sign):
        return summary_slot(4 * ((z + shift[1]) % 2) + (x + 4 + sign * shift[0]) % 4)

    for shift, piece in zip(SHIFTS, spread):
        bank[slot_at(shift, -1)] = piece[...]
    bank[EDGE] = edge[...]
    for g in range(8):
        y, row = (g, 0) if g < 4 else (7 - g, BLK)
        for kind in range(2):
            bank[OWN + g, kind] = recv_kv[y, kind, row : row + BLK, :]

    def clear(slot, carry):
        grad_bank[slot] = jnp.zeros(grad_bank.shape[1:], F32)
        return carry

    lax.fori_loop(0, SLOTS, clear, 0)
    causal = lax.broadcasted_iota(jnp.int32, (BLK, BLK), 0) >= lax.broadcasted_iota(
        jnp.int32, (BLK, BLK), 1
    )

    def one_block(g, carry):
        lower = g < 4
        y = jnp.where(lower, g, 7 - g)
        row = pl.multiple_of(jnp.where(lower, 0, BLK), BLK)
        block = jnp.where(lower, 4 * c + g, 56 - 4 * c + g)
        outside = jnp.where(
            lower,
            jnp.where(c % 2 == 0, jnp.maximum(c // 2 - 1, 0), EDGE),
            jnp.where(c % 2 == 0, EDGE, (13 - c) // 2),
        )
        prev = jnp.where(g % 4 == 0, outside, OWN + g - 1)
        slots = [prev, OWN + g]
        bias = [jnp.where(block >= 1, 0.0, NEG), None]
        for p in range(PICKS):
            pick = lists[block, p]
            slots.append(pick)
            bias.append(jnp.where(8 * pick + 7 < block - 1, 0.0, NEG))

        def products(h):
            cols = slice(h * HS, (h + 1) * HS)
            query = recv[y, 0, pl.ds(row, BLK), cols]
            grad = recv[y, 1, pl.ds(row, BLK), cols]
            key_rows = jnp.concatenate([bank[s, 0, :, cols] for s in slots], axis=0)
            value_rows = jnp.concatenate([bank[s, 1, :, cols] for s in slots], axis=0)
            return nt(query, key_rows) * SCALE, nt(grad, value_rows)

        def soften(scores, dprob):
            pieces = []
            for i in range(2 + PICKS):
                piece = scores[:, i * BLK : (i + 1) * BLK]
                if bias[i] is None:
                    pieces.append(jnp.where(causal, piece, NEG))
                else:
                    pieces.append(piece + bias[i])
            scores = jnp.concatenate(pieces, axis=1)
            weights = jnp.exp(scores - jnp.max(scores, axis=1, keepdims=True))
            inverse = 1.0 / jnp.sum(weights, axis=1, keepdims=True)
            delta = jnp.sum(weights * dprob, axis=1, keepdims=True) * inverse
            probs = weights * inverse
            return probs.astype(BF16), (probs * (dprob - delta)).astype(BF16)

        def results(h, probs_low, dscore):
            cols = slice(h * HS, (h + 1) * HS)
            query = recv[y, 0, pl.ds(row, BLK), cols]
            grad = recv[y, 1, pl.ds(row, BLK), cols]
            key_rows = jnp.concatenate([bank[s, 0, :, cols] for s in slots], axis=0)
            value_rows = jnp.concatenate([bank[s, 1, :, cols] for s in slots], axis=0)
            out[y, 0, pl.ds(row, BLK), cols] = nn(probs_low, value_rows).astype(BF16)
            out[y, 1, pl.ds(row, BLK), cols] = (nn(dscore, key_rows) * SCALE).astype(BF16)
            grad_keys = nn(query.T, dscore)
            grad_values = nn(grad.T, probs_low)
            for i, s in enumerate(slots):
                at = slice(i * BLK, (i + 1) * BLK)
                grad_bank[s, 0, h] += grad_keys[:, at]
                grad_bank[s, 1, h] += grad_values[:, at]

        first = products(0)
        second = products(1)
        soft = soften(*first)
        third = products(2)
        results(0, *soft)
        soft = soften(*second)
        results(1, *soft)
        soft = soften(*third)
        results(2, *soft)
        return carry

    lax.fori_loop(0, 8, one_block, 0)

    def taken(slot, kind, h):
        total = grad_bank[slot, kind, h]
        if kind == 0:
            total = total * SCALE
        return total.T.astype(BF16)

    def finish(g, carry):
        lower = g < 4
        y = jnp.where(lower, g, 7 - g)
        row = pl.multiple_of(jnp.where(lower, 0, BLK), BLK)
        for kind in range(2):
            for h in range(HEADS):
                cols = slice(h * HS, (h + 1) * HS)
                out[y, 2 + kind, pl.ds(row, BLK), cols] = taken(OWN + g, kind, h)
        return carry

    lax.fori_loop(0, 8, finish, 0)
    for kind in range(2):
        for h in range(HEADS):
            cols = slice(h * HS, (h + 1) * HS)
            edge_out[kind, :, cols] = taken(EDGE, kind, h)
            for shift, part in zip(SHIFTS, parts):
                part[kind, :, cols] = taken(slot_at(shift, 1), kind, h)


def attend(place, lists, recv_kv, recv, spread, edge):
    vmem = pl.BlockSpec(memory_space=pltpu.VMEM)
    smem = pl.BlockSpec(memory_space=pltpu.SMEM)
    piece = jax.ShapeDtypeStruct((2, BLK, COLS), BF16)
    outs = pl.pallas_call(
        attend_kernel,
        in_specs=[smem, smem] + [vmem] * 11,
        out_specs=[vmem] * 10,
        out_shape=[jax.ShapeDtypeStruct((RING, 4, 2 * BLK, COLS), BF16)] + [piece] * 9,
        scratch_shapes=[
            pltpu.VMEM((SLOTS, 2, BLK, COLS), BF16),
            pltpu.VMEM((SLOTS, 2, HEADS, HS, BLK), F32),
        ],
        name="attend",
    )(place, lists, recv_kv, recv, *spread, edge)
    return outs[0], outs[1:9], outs[9]


def unpack_kernel(place, recv, own, one, two, three, out, grad_q, grad_k, grad_v):
    y = place[0] % 4
    step = pl.program_id(0)
    out[...] = recv[0, 0]
    grad_q[...] = recv[0, 1]
    grad_k[...] = recv[0, 2]
    grad_v[...] = recv[0, 3]
    for end, row in ((3, 0), (0, BLK)):
        for i, extra in enumerate((own, one, two, three)):

            @pl.when((y == end) & (step == (y + i) % 4))
            def _():
                for kind, grad in ((0, grad_k), (1, grad_v)):
                    total = recv[0, 2 + kind, row : row + BLK].astype(F32)
                    grad[row : row + BLK] = (total + extra[kind].astype(F32)).astype(BF16)


def unpack(place, recv, extras):
    rows = recv.shape[2]
    whole = pl.BlockSpec((2, BLK, COLS), lambda i, place: (0, 0, 0))
    return pl.pallas_call(
        unpack_kernel,
        grid_spec=pltpu.PrefetchScalarGridSpec(
            num_scalar_prefetch=1,
            grid=(RING,),
            in_specs=[pl.BlockSpec((1, 4, rows, COLS), lambda i, place: (i, 0, 0, 0))]
            + [whole] * 4,
            out_specs=[pl.BlockSpec((rows, COLS), lambda i, place: (0, i))] * 4,
        ),
        out_shape=[jax.ShapeDtypeStruct((rows, H * HS), BF16)] * 4,
        name="unpack",
    )(place, recv, *extras)


def on_device(queries, keys, values, grad_out, summary_lists):
    here = lax.axis_index("ctx").astype(jnp.int32)
    place = here[None]
    c, y = here // 4, here % 4
    from_summary = (y - 3 * (c % 2)) % 4

    def ring_exchange(sent):
        return lax.all_to_all(sent, "ctx", 0, 0, axis_index_groups=RING_GROUPS)

    recv_kv = ring_exchange(pack(keys, values))
    recv = ring_exchange(pack(queries, grad_out))
    odd = c % 2 == 1
    ends = recv_kv[3, :, :BLK], recv_kv[0, :, BLK:]
    summary = jnp.where(odd, ends[0], ends[1])
    edge = lax.ppermute(jnp.where(odd, ends[1], ends[0]), "ctx", edge_pairs())
    spread = [summary] + [lax.ppermute(summary, "ctx", spread_pairs(s)) for s in SHIFTS[1:]]

    back, parts, edge_grad = attend(place, summary_lists, recv_kv, recv, spread, edge)

    total = parts[0].astype(F32)
    for part, shift in zip(parts[1:], SHIFTS[1:]):
        total = total + lax.ppermute(part, "ctx", reduce_pairs(shift)).astype(F32)
    total = total.astype(BF16)
    edge_total = lax.ppermute(edge_grad, "ctx", edge_pairs())
    home = ring_exchange(back)
    extras = [jnp.where(from_summary == 0, total, edge_total)]
    for k in range(1, 4):
        mine = jnp.where(from_summary == k, total, edge_total)
        extras.append(lax.ppermute(mine, "ctx", return_pairs(k)))
    return tuple(unpack(place, home, extras))


def solution(mesh):
    rows = P(("dp", "ctx"), None)
    return jax.shard_map(
        on_device,
        mesh=mesh,
        in_specs=(rows, rows, rows, rows, P("dp", None)),
        out_specs=(rows, rows, rows, rows),
        check_vma=False,
    )
```

```python
import jax
import jax.numpy as jnp
from jax import lax
from jax.experimental import pallas as pl
from jax.experimental.pallas import tpu as pltpu
from jax.sharding import PartitionSpec as P

H = 12
HS = 128
BLK = 128
SUMS = 8
PICKS = 4
N_CTX = 32
RING = 4
GROUPS = N_CTX // RING
HEADS = H // RING
COLS = HEADS * HS
EDGE = SUMS
OWN = SUMS + 1
SLOTS = OWN + 2 * RING
SCALE = HS ** (-0.5)
NEG = -1e30
BF16 = jnp.bfloat16
F32 = jnp.float32


RING_GROUPS = [[RING * c + y for y in range(RING)] for c in range(GROUPS)]
FLIPS = (1, 6, 7, 2, 5, 3, 4)


def summary_y(c):
    return 3 * (c % 2)


def edge_y(c):
    return 3 - 3 * (c % 2)


def summary_of(c):
    return (c - 1) // 2 if c % 2 else 7 - c // 2


def uses(c, source):
    return 8 * summary_of(source) + 9 <= 63 - 4 * c


def return_pairs(k):
    pairs = []
    for c in range(GROUPS):
        for end in (summary_y(c), edge_y(c)):
            pairs.append((4 * c + (end + k) % 4, 4 * c + end))
    return pairs


def flip_pairs(flip, forward):
    pairs = []
    for c in range(GROUPS):
        source, user = (c, c ^ flip) if forward else (c ^ flip, c)
        if flip == 1 or uses(user, source):
            pairs += [(4 * c + y, 4 * (c ^ flip) + y) for y in range(RING)]
    return pairs


def pack_kernel(first, second, out, held, sems):
    def copies(i, j, source):
        fetch = pltpu.make_async_copy(
            source.at[:, i * COLS : (i + 1) * COLS], held.at[i, j], sems.at[0, i, j]
        )
        return fetch, pltpu.make_async_copy(held.at[i, j], out.at[i, j], sems.at[1, i, j])

    steps = [
        copies(i, j, source) for i in range(RING) for j, source in enumerate((first, second))
    ]
    for fetch, _ in steps:
        fetch.start()
    for fetch, store in steps:
        fetch.wait()
        store.start()
    for _, store in steps:
        store.wait()


def pack(first, second):
    rows = first.shape[0]
    anywhere = pl.BlockSpec(memory_space=pl.ANY)
    return pl.pallas_call(
        pack_kernel,
        in_specs=[anywhere] * 2,
        out_specs=anywhere,
        out_shape=jax.ShapeDtypeStruct((RING, 2, rows, COLS), BF16),
        scratch_shapes=[
            pltpu.VMEM((RING, 2, rows, COLS), BF16),
            pltpu.SemaphoreType.DMA((2, RING, 2)),
        ],
        name="pack",
    )(first, second)


def summary_slot(c):
    return jnp.where(c % 2 == 1, (c - 1) // 2, 7 - c // 2)


def nt(a, b):
    return lax.dot_general(a, b, (((1,), (1,)), ((), ())), preferred_element_type=F32)


def nn(a, b):
    return lax.dot_general(a, b, (((1,), (0,)), ((), ())), preferred_element_type=F32)


def attend_kernel(place, lists, recv_kv, recv, *refs):
    own, got, near = refs[0], refs[1:7], refs[7]
    out, own_part, parts, near_part = refs[8], refs[9], refs[10:16], refs[16]
    bank, grad_bank = refs[17], refs[18]
    c = place[0] // 4
    bank[summary_slot(c)] = own[...]
    for flip, piece in zip(FLIPS[1:], got):
        bank[summary_slot(c ^ flip)] = piece[...]
    bank[summary_slot(c ^ 1)] = near[0]
    bank[EDGE] = near[1]
    for g in range(8):
        y, row = (g, 0) if g < 4 else (7 - g, BLK)
        for kind in range(2):
            bank[OWN + g, kind] = recv_kv[y, kind, row : row + BLK, :]

    def clear(slot, carry):
        grad_bank[slot] = jnp.zeros(grad_bank.shape[1:], F32)
        return carry

    lax.fori_loop(0, SLOTS, clear, 0)
    causal = lax.broadcasted_iota(jnp.int32, (BLK, BLK), 0) >= lax.broadcasted_iota(
        jnp.int32, (BLK, BLK), 1
    )

    def one_block(g, carry):
        lower = g < 4
        y = jnp.where(lower, g, 7 - g)
        row = pl.multiple_of(jnp.where(lower, 0, BLK), BLK)
        block = jnp.where(lower, 4 * c + g, 56 - 4 * c + g)
        outside = jnp.where(
            lower,
            jnp.where(c % 2 == 0, jnp.maximum(c // 2 - 1, 0), EDGE),
            jnp.where(c % 2 == 0, EDGE, (13 - c) // 2),
        )
        prev = jnp.where(g % 4 == 0, outside, OWN + g - 1)
        slots = [prev, OWN + g]
        bias = [jnp.where(block >= 1, 0.0, NEG), None]
        for p in range(PICKS):
            pick = lists[block, p]
            slots.append(pick)
            bias.append(jnp.where(8 * pick + 7 < block - 1, 0.0, NEG))

        def products(h):
            cols = slice(h * HS, (h + 1) * HS)
            query = recv[y, 0, pl.ds(row, BLK), cols]
            grad = recv[y, 1, pl.ds(row, BLK), cols]
            key_rows = jnp.concatenate([bank[s, 0, :, cols] for s in slots], axis=0)
            value_rows = jnp.concatenate([bank[s, 1, :, cols] for s in slots], axis=0)
            return nt(query, key_rows) * SCALE, nt(grad, value_rows)

        def soften(scores, dprob):
            pieces = []
            for i in range(2 + PICKS):
                piece = scores[:, i * BLK : (i + 1) * BLK]
                if bias[i] is None:
                    pieces.append(jnp.where(causal, piece, NEG))
                else:
                    pieces.append(piece + bias[i])
            scores = jnp.concatenate(pieces, axis=1)
            weights = jnp.exp(scores - jnp.max(scores, axis=1, keepdims=True))
            inverse = 1.0 / jnp.sum(weights, axis=1, keepdims=True)
            delta = jnp.sum(weights * dprob, axis=1, keepdims=True) * inverse
            probs = weights * inverse
            return probs.astype(BF16), (probs * (dprob - delta)).astype(BF16)

        def results(h, probs_low, dscore):
            cols = slice(h * HS, (h + 1) * HS)
            query = recv[y, 0, pl.ds(row, BLK), cols]
            grad = recv[y, 1, pl.ds(row, BLK), cols]
            key_rows = jnp.concatenate([bank[s, 0, :, cols] for s in slots], axis=0)
            value_rows = jnp.concatenate([bank[s, 1, :, cols] for s in slots], axis=0)
            out[y, 0, pl.ds(row, BLK), cols] = nn(probs_low, value_rows).astype(BF16)
            out[y, 1, pl.ds(row, BLK), cols] = (nn(dscore, key_rows) * SCALE).astype(BF16)
            grad_keys = nn(query.T, dscore)
            grad_values = nn(grad.T, probs_low)
            for i, s in enumerate(slots):
                at = slice(i * BLK, (i + 1) * BLK)
                grad_bank[s, 0, h] += grad_keys[:, at]
                grad_bank[s, 1, h] += grad_values[:, at]

        first = products(0)
        second = products(1)
        soft = soften(*first)
        third = products(2)
        results(0, *soft)
        soft = soften(*second)
        results(1, *soft)
        soft = soften(*third)
        results(2, *soft)
        return carry

    lax.fori_loop(0, 8, one_block, 0)

    def taken(slot, kind, h):
        total = grad_bank[slot, kind, h]
        if kind == 0:
            total = total * SCALE
        return total.T.astype(BF16)

    def finish(g, carry):
        lower = g < 4
        y = jnp.where(lower, g, 7 - g)
        row = pl.multiple_of(jnp.where(lower, 0, BLK), BLK)
        for kind in range(2):
            for h in range(HEADS):
                cols = slice(h * HS, (h + 1) * HS)
                out[y, 2 + kind, pl.ds(row, BLK), cols] = taken(OWN + g, kind, h)
        return carry

    lax.fori_loop(0, 8, finish, 0)
    for kind in range(2):
        for h in range(HEADS):
            cols = slice(h * HS, (h + 1) * HS)
            near_part[0, kind, :, cols] = taken(summary_slot(c ^ 1), kind, h)
            near_part[1, kind, :, cols] = taken(EDGE, kind, h)
            own_part[kind, :, cols] = taken(summary_slot(c), kind, h)
            for flip, part in zip(FLIPS[1:], parts):
                part[kind, :, cols] = taken(summary_slot(c ^ flip), kind, h)


def attend(place, lists, recv_kv, recv, own, got, near):
    vmem = pl.BlockSpec(memory_space=pltpu.VMEM)
    smem = pl.BlockSpec(memory_space=pltpu.SMEM)
    piece = jax.ShapeDtypeStruct((2, BLK, COLS), BF16)
    pair = jax.ShapeDtypeStruct((2, 2, BLK, COLS), BF16)
    outs = pl.pallas_call(
        attend_kernel,
        in_specs=[smem, smem] + [vmem] * 10,
        out_specs=[vmem] * 9,
        out_shape=[jax.ShapeDtypeStruct((RING, 4, 2 * BLK, COLS), BF16)] + [piece] * 7 + [pair],
        scratch_shapes=[
            pltpu.VMEM((SLOTS, 2, BLK, COLS), BF16),
            pltpu.VMEM((SLOTS, 2, HEADS, HS, BLK), F32),
        ],
        name="attend",
    )(place, lists, recv_kv, recv, own, *got, near)
    return outs[0], outs[1], outs[2:8], outs[8]


def unpack_kernel(place, recv, own, one, two, three, out, grad_q, grad_k, grad_v, held, sems):
    y = place[0] % 4
    extras = (own, one, two, three)

    def cols(i):
        return slice((i % RING) * COLS, (i % RING + 1) * COLS)

    copies = [
        pltpu.make_async_copy(recv.at[i, j], target.at[:, cols(i)], sems.at[j, i])
        for i in range(RING)
        for j, target in enumerate((out, grad_q))
    ]
    for copy in copies:
        copy.start()
    for kind in range(2):
        for i in range(RING):
            held[kind, :, cols(i)] = recv[i, 2 + kind]
    for end, row in ((3, 0), (0, BLK)):

        @pl.when(y == end)
        def _():
            rows = slice(row, row + BLK)
            for kind in range(2):
                for i, extra in enumerate(extras):
                    total = recv[(end + i) % RING, 2 + kind, rows, :].astype(F32)
                    total = total + extra[kind].astype(F32)
                    held[kind, rows, cols(end + i)] = total.astype(BF16)

    late = [
        pltpu.make_async_copy(held.at[kind], target, sems.at[2 + kind, 0])
        for kind, target in enumerate((grad_k, grad_v))
    ]
    for copy in late:
        copy.start()
    for copy in copies + late:
        copy.wait()


def unpack(place, recv, extras):
    rows = recv.shape[2]
    vmem = pl.BlockSpec(memory_space=pltpu.VMEM)
    return pl.pallas_call(
        unpack_kernel,
        in_specs=[pl.BlockSpec(memory_space=pltpu.SMEM)] + [vmem] * 5,
        out_specs=[pl.BlockSpec(memory_space=pl.ANY)] * 4,
        out_shape=[jax.ShapeDtypeStruct((rows, H * HS), BF16)] * 4,
        scratch_shapes=[
            pltpu.VMEM((2, rows, H * HS), BF16),
            pltpu.SemaphoreType.DMA((4, RING)),
        ],
        name="unpack",
    )(place, recv, *extras)


def on_device(queries, keys, values, grad_out, summary_lists):
    here = lax.axis_index("ctx").astype(jnp.int32)
    place = here[None]
    c, y = here // 4, here % 4
    from_summary = (y - 3 * (c % 2)) % 4

    def ring_exchange(sent):
        return lax.all_to_all(sent, "ctx", 0, 0, axis_index_groups=RING_GROUPS)

    recv_kv = ring_exchange(pack(keys, values))
    recv = ring_exchange(pack(queries, grad_out))
    odd = c % 2 == 1
    ends = recv_kv[3, :, :BLK], recv_kv[0, :, BLK:]
    summary = jnp.where(odd, ends[0], ends[1])
    near = jnp.stack([summary, jnp.where(odd, ends[1], ends[0])])

    def flipped(value, flip, forward):
        return lax.ppermute(value, "ctx", flip_pairs(flip, forward))

    near = flipped(near, 1, True)
    got = [flipped(summary, flip, True) for flip in FLIPS[1:]]

    back, own_part, parts, near_part = attend(
        place, summary_lists, recv_kv, recv, summary, got, near
    )

    near_part = flipped(near_part, 1, False)
    total = own_part.astype(F32) + near_part[0].astype(F32)
    for part, flip in zip(parts, FLIPS[1:]):
        total = total + flipped(part, flip, False).astype(F32)
    total = total.astype(BF16)
    edge_total = near_part[1]
    home = ring_exchange(back)
    extras = [jnp.where(from_summary == 0, total, edge_total)]
    for k in range(1, 4):
        mine = jnp.where(from_summary == k, total, edge_total)
        extras.append(lax.ppermute(mine, "ctx", return_pairs(k)))
    return tuple(unpack(place, home, extras))


def solution(mesh):
    rows = P(("dp", "ctx"), None)
    return jax.shard_map(
        on_device,
        mesh=mesh,
        in_specs=(rows, rows, rows, rows, P("dp", None)),
        out_specs=(rows, rows, rows, rows),
        check_vma=False,
    )
```

```python
import jax
import jax.numpy as jnp
from jax import lax
from jax.experimental import pallas as pl
from jax.experimental.pallas import tpu as pltpu
from jax.sharding import PartitionSpec as P

H = 12
HS = 128
BLK = 128
SUMS = 8
PICKS = 4
N_CTX = 32
RING = 4
GROUPS = N_CTX // RING
HEADS = H // RING
COLS = HEADS * HS
EDGE = SUMS
OWN = SUMS + 1
SLOTS = OWN + 2 * RING
SCALE = HS ** (-0.5)
NEG = -1e30
BF16 = jnp.bfloat16
F32 = jnp.float32


RING_GROUPS = [[RING * c + y for y in range(RING)] for c in range(GROUPS)]
FLIPS = (1, 6, 7, 2, 5, 3, 4)


def summary_y(c):
    return 3 * (c % 2)


def edge_y(c):
    return 3 - 3 * (c % 2)


def summary_of(c):
    return (c - 1) // 2 if c % 2 else 7 - c // 2


def uses(c, source):
    return 8 * summary_of(source) + 9 <= 63 - 4 * c


def return_pairs(k):
    pairs = []
    for c in range(GROUPS):
        for end in (summary_y(c), edge_y(c)):
            pairs.append((4 * c + (end + k) % 4, 4 * c + end))
    return pairs


def flip_pairs(flip, forward):
    pairs = []
    for c in range(GROUPS):
        source, user = (c, c ^ flip) if forward else (c ^ flip, c)
        if flip == 1 or uses(user, source):
            pairs += [(4 * c + y, 4 * (c ^ flip) + y) for y in range(RING)]
    return pairs


def pack_kernel(first, second, out, held, sems):
    def copies(i, j, source):
        fetch = pltpu.make_async_copy(
            source.at[:, i * COLS : (i + 1) * COLS], held.at[i, j], sems.at[0, i, j]
        )
        return fetch, pltpu.make_async_copy(held.at[i, j], out.at[i, j], sems.at[1, i, j])

    steps = [
        copies(i, j, source) for i in range(RING) for j, source in enumerate((first, second))
    ]
    for fetch, _ in steps:
        fetch.start()
    for fetch, store in steps:
        fetch.wait()
        store.start()
    for _, store in steps:
        store.wait()


def pack(first, second):
    rows = first.shape[0]
    anywhere = pl.BlockSpec(memory_space=pl.ANY)
    return pl.pallas_call(
        pack_kernel,
        in_specs=[anywhere] * 2,
        out_specs=anywhere,
        out_shape=jax.ShapeDtypeStruct((RING, 2, rows, COLS), BF16),
        scratch_shapes=[
            pltpu.VMEM((RING, 2, rows, COLS), BF16),
            pltpu.SemaphoreType.DMA((2, RING, 2)),
        ],
        name="pack",
    )(first, second)


def summary_slot(c):
    return jnp.where(c % 2 == 1, (c - 1) // 2, 7 - c // 2)


def resident(array):
    return pltpu.with_memory_space_constraint(array, pltpu.VMEM)


def nt(a, b):
    return lax.dot_general(a, b, (((1,), (1,)), ((), ())), preferred_element_type=F32)


def nn(a, b):
    return lax.dot_general(a, b, (((1,), (0,)), ((), ())), preferred_element_type=F32)


def attend_kernel(place, lists, recv_kv, recv, *refs):
    own, got, near = refs[0], refs[1:7], refs[7]
    out, own_part, parts, near_part = refs[8], refs[9], refs[10:16], refs[16]
    bank, grad_bank = refs[17], refs[18]
    c = place[0] // 4
    bank[summary_slot(c)] = own[...]
    for flip, piece in zip(FLIPS[1:], got):
        bank[summary_slot(c ^ flip)] = piece[...]
    bank[summary_slot(c ^ 1)] = near[0]
    bank[EDGE] = near[1]
    for g in range(8):
        y, row = (g, 0) if g < 4 else (7 - g, BLK)
        for kind in range(2):
            bank[OWN + g, kind] = recv_kv[y, kind, row : row + BLK, :]

    def clear(slot, carry):
        grad_bank[slot] = jnp.zeros(grad_bank.shape[1:], F32)
        return carry

    lax.fori_loop(0, SLOTS, clear, 0)
    causal = lax.broadcasted_iota(jnp.int32, (BLK, BLK), 0) >= lax.broadcasted_iota(
        jnp.int32, (BLK, BLK), 1
    )

    def one_block(g, carry):
        lower = g < 4
        y = jnp.where(lower, g, 7 - g)
        row = pl.multiple_of(jnp.where(lower, 0, BLK), BLK)
        block = jnp.where(lower, 4 * c + g, 56 - 4 * c + g)
        outside = jnp.where(
            lower,
            jnp.where(c % 2 == 0, jnp.maximum(c // 2 - 1, 0), EDGE),
            jnp.where(c % 2 == 0, EDGE, (13 - c) // 2),
        )
        prev = jnp.where(g % 4 == 0, outside, OWN + g - 1)
        slots = [prev, OWN + g]
        bias = [jnp.where(block >= 1, 0.0, NEG), None]
        for p in range(PICKS):
            pick = lists[block, p]
            slots.append(pick)
            bias.append(jnp.where(8 * pick + 7 < block - 1, 0.0, NEG))

        def products(h):
            cols = slice(h * HS, (h + 1) * HS)
            query = recv[y, 0, pl.ds(row, BLK), cols]
            grad = recv[y, 1, pl.ds(row, BLK), cols]
            key_rows = jnp.concatenate([bank[s, 0, :, cols] for s in slots], axis=0)
            value_rows = jnp.concatenate([bank[s, 1, :, cols] for s in slots], axis=0)
            return nt(query, key_rows) * SCALE, nt(grad, value_rows)

        def soften(scores, dprob):
            pieces = []
            for i in range(2 + PICKS):
                piece = scores[:, i * BLK : (i + 1) * BLK]
                if bias[i] is None:
                    pieces.append(jnp.where(causal, piece, NEG))
                else:
                    pieces.append(piece + bias[i])
            scores = jnp.concatenate(pieces, axis=1)
            weights = jnp.exp(scores - jnp.max(scores, axis=1, keepdims=True))
            inverse = 1.0 / jnp.sum(weights, axis=1, keepdims=True)
            delta = jnp.sum(weights * dprob, axis=1, keepdims=True) * inverse
            probs = weights * inverse
            return probs.astype(BF16), (probs * (dprob - delta)).astype(BF16)

        def results(h, probs_low, dscore):
            cols = slice(h * HS, (h + 1) * HS)
            query = recv[y, 0, pl.ds(row, BLK), cols]
            grad = recv[y, 1, pl.ds(row, BLK), cols]
            key_rows = jnp.concatenate([bank[s, 0, :, cols] for s in slots], axis=0)
            value_rows = jnp.concatenate([bank[s, 1, :, cols] for s in slots], axis=0)
            out[y, 0, pl.ds(row, BLK), cols] = nn(probs_low, value_rows).astype(BF16)
            out[y, 1, pl.ds(row, BLK), cols] = (nn(dscore, key_rows) * SCALE).astype(BF16)
            grad_keys = nn(query.T, dscore)
            grad_values = nn(grad.T, probs_low)
            for i, s in enumerate(slots):
                at = slice(i * BLK, (i + 1) * BLK)
                grad_bank[s, 0, h] += grad_keys[:, at]
                grad_bank[s, 1, h] += grad_values[:, at]

        first = products(0)
        second = products(1)
        soft = soften(*first)
        third = products(2)
        results(0, *soft)
        soft = soften(*second)
        results(1, *soft)
        soft = soften(*third)
        results(2, *soft)
        return carry

    lax.fori_loop(0, 8, one_block, 0)

    def taken(slot, kind, h):
        total = grad_bank[slot, kind, h]
        if kind == 0:
            total = total * SCALE
        return total.T.astype(BF16)

    def finish(g, carry):
        lower = g < 4
        y = jnp.where(lower, g, 7 - g)
        row = pl.multiple_of(jnp.where(lower, 0, BLK), BLK)
        for kind in range(2):
            for h in range(HEADS):
                cols = slice(h * HS, (h + 1) * HS)
                out[y, 2 + kind, pl.ds(row, BLK), cols] = taken(OWN + g, kind, h)
        return carry

    lax.fori_loop(0, 8, finish, 0)
    for kind in range(2):
        for h in range(HEADS):
            cols = slice(h * HS, (h + 1) * HS)
            near_part[0, kind, :, cols] = taken(summary_slot(c ^ 1), kind, h)
            near_part[1, kind, :, cols] = taken(EDGE, kind, h)
            own_part[kind, :, cols] = taken(summary_slot(c), kind, h)
            for flip, part in zip(FLIPS[1:], parts):
                part[kind, :, cols] = taken(summary_slot(c ^ flip), kind, h)


def attend(place, lists, recv_kv, recv, own, got, near):
    vmem = pl.BlockSpec(memory_space=pltpu.VMEM)
    smem = pl.BlockSpec(memory_space=pltpu.SMEM)
    piece = jax.ShapeDtypeStruct((2, BLK, COLS), BF16)
    pair = jax.ShapeDtypeStruct((2, 2, BLK, COLS), BF16)
    outs = pl.pallas_call(
        attend_kernel,
        in_specs=[smem, smem] + [vmem] * 10,
        out_specs=[vmem] * 9,
        out_shape=[jax.ShapeDtypeStruct((RING, 4, 2 * BLK, COLS), BF16)] + [piece] * 7 + [pair],
        scratch_shapes=[
            pltpu.VMEM((SLOTS, 2, BLK, COLS), BF16),
            pltpu.VMEM((SLOTS, 2, HEADS, HS, BLK), F32),
        ],
        compiler_params=pltpu.CompilerParams(vmem_limit_bytes=54 << 20),
        name="attend",
    )(place, lists, *[resident(a) for a in (recv_kv, recv, own, *got, near)])
    return outs[0], outs[1], outs[2:8], outs[8]


def unpack_kernel(place, recv, own, one, two, three, out, grad_q, grad_k, grad_v, held, sems):
    y = place[0] % 4
    extras = (own, one, two, three)

    def cols(i):
        return slice((i % RING) * COLS, (i % RING + 1) * COLS)

    copies = [
        pltpu.make_async_copy(recv.at[i, j], target.at[:, cols(i)], sems.at[j, i])
        for i in range(RING)
        for j, target in enumerate((out, grad_q))
    ]
    for copy in copies:
        copy.start()
    for kind in range(2):
        for i in range(RING):
            held[kind, :, cols(i)] = recv[i, 2 + kind]
    for end, row in ((3, 0), (0, BLK)):

        @pl.when(y == end)
        def _():
            rows = slice(row, row + BLK)
            for kind in range(2):
                for i, extra in enumerate(extras):
                    total = recv[(end + i) % RING, 2 + kind, rows, :].astype(F32)
                    total = total + extra[kind].astype(F32)
                    held[kind, rows, cols(end + i)] = total.astype(BF16)

    late = [
        pltpu.make_async_copy(held.at[kind], target, sems.at[2 + kind, 0])
        for kind, target in enumerate((grad_k, grad_v))
    ]
    for copy in late:
        copy.start()
    for copy in copies + late:
        copy.wait()


def unpack(place, recv, extras):
    rows = recv.shape[2]
    vmem = pl.BlockSpec(memory_space=pltpu.VMEM)
    return pl.pallas_call(
        unpack_kernel,
        in_specs=[pl.BlockSpec(memory_space=pltpu.SMEM)] + [vmem] * 5,
        out_specs=[pl.BlockSpec(memory_space=pl.ANY)] * 4,
        out_shape=[jax.ShapeDtypeStruct((rows, H * HS), BF16)] * 4,
        scratch_shapes=[
            pltpu.VMEM((2, rows, H * HS), BF16),
            pltpu.SemaphoreType.DMA((4, RING)),
        ],
        compiler_params=pltpu.CompilerParams(vmem_limit_bytes=16 << 20),
        name="unpack",
    )(place, resident(recv), *extras)


def on_device(queries, keys, values, grad_out, summary_lists):
    here = lax.axis_index("ctx").astype(jnp.int32)
    place = here[None]
    c, y = here // 4, here % 4
    from_summary = (y - 3 * (c % 2)) % 4

    def ring_exchange(sent):
        return lax.all_to_all(sent, "ctx", 0, 0, axis_index_groups=RING_GROUPS)

    recv_kv = ring_exchange(pack(keys, values))
    recv = ring_exchange(pack(queries, grad_out))
    odd = c % 2 == 1
    ends = recv_kv[3, :, :BLK], recv_kv[0, :, BLK:]
    summary = jnp.where(odd, ends[0], ends[1])
    near = jnp.stack([summary, jnp.where(odd, ends[1], ends[0])])

    def flipped(value, flip, forward):
        return lax.ppermute(value, "ctx", flip_pairs(flip, forward))

    near = flipped(near, 1, True)
    got = [flipped(summary, flip, True) for flip in FLIPS[1:]]

    back, own_part, parts, near_part = attend(
        place, summary_lists, recv_kv, recv, summary, got, near
    )

    near_part = flipped(near_part, 1, False)
    total = own_part.astype(F32) + near_part[0].astype(F32)
    for part, flip in zip(parts, FLIPS[1:]):
        total = total + flipped(part, flip, False).astype(F32)
    total = total.astype(BF16)
    edge_total = near_part[1]
    home = ring_exchange(back)
    extras = [jnp.where(from_summary == 0, total, edge_total)]
    for k in range(1, 4):
        mine = jnp.where(from_summary == k, total, edge_total)
        extras.append(lax.ppermute(mine, "ctx", return_pairs(k)))
    return tuple(unpack(place, home, extras))


def solution(mesh):
    rows = P(("dp", "ctx"), None)
    return jax.shard_map(
        on_device,
        mesh=mesh,
        in_specs=(rows, rows, rows, rows, P("dp", None)),
        out_specs=(rows, rows, rows, rows),
        check_vma=False,
    )
```
